32 devices in a mesh: epoch: 4 (over y, x), sky: 8 (over z, core).
Axes of the slice: x: 2, y: 2, z: 4, core: 2. Of those that a mesh axis runs over, the one named last changes fastest.
Arguments:
- image: bfloat16 [16, 384, 2048], P('epoch', 'sky'), may hold values from -400 to 400
- inv_variance: bfloat16 [16, 384, 2048], P('epoch', 'sky'), may hold values from 0.25 to 4
- psf_rows: float32 [9], replicated, may hold values from 0.05 to 1
- psf_cols: float32 [9], replicated, may hold values from 0.05 to 1
- shift_num: int32 [4, 16], replicated, may hold values from -64 to 64, as said below
Outputs:
- search_map: float32 [384, 2048], P('sky', 'epoch')
The draws below stay inside these ranges and needn't reach their ends.
Inputs may be any that keep to these rules, and one draw needn't show every extreme that they name: `shift_num`: at level l every entry has magnitude at most 4 * 2 * 2^l, and at each level some entry equals plus and some other entry minus that bound.
All inputs are finite; a program needn't handle non-finite values.
Results may differ from the reference program's by a relative error of at most 0.0024.
Values may be sent and summed in bfloat16 or wider, within the bound.
A program may use at most 64 MiB of HBM per device.

```python
import math
import jax
import jax.numpy as jnp
from jax import lax

EPOCHS = 16
LEVELS = 4
COLS = 2048
PSF_HALF = 4
DEN = 4
VMAX = 2
ROWS = 384


def draw_image(key, part):
    key_base = jax.random.fold_in(jax.random.fold_in(key, 11), 0)
    base_values = jax.random.normal(key_base, (EPOCHS, ROWS, COLS), jnp.float32)
    return jnp.clip(base_values, -6.0, 6.0).astype(jnp.bfloat16)


def draw_shift_num(key, part):
    key_raw, key_top, key_low = jax.random.split(jax.random.fold_in(key, 23), 3)
    limits = DEN * VMAX * (2 ** jnp.arange(LEVELS, dtype=jnp.int32))[:, None]
    raw_values = jax.random.randint(key_raw, (LEVELS, EPOCHS), 0, 1 << 20, dtype=jnp.int32)
    values = raw_values % (2 * limits + 1) - limits
    column = jnp.arange(EPOCHS, dtype=jnp.int32)[None, :]
    top_pos = jax.random.randint(key_top, (LEVELS, 1), 0, EPOCHS, dtype=jnp.int32)
    low_pos = (top_pos + 1 + jax.random.randint(key_low, (LEVELS, 1), 0, EPOCHS - 1, dtype=jnp.int32)) % EPOCHS
    values = jnp.where(column == top_pos, limits, jnp.where(column == low_pos, -limits, values))
    return values.astype(jnp.int32)


def levels(stream_key, extent, cuts, least, top_value):
    def one(dim, blocks):
        steps = jax.random.uniform(jax.random.fold_in(jax.random.fold_in(stream_key, 6), dim), (blocks,), jnp.float32, least / len(cuts), top_value / len(cuts))
        return jnp.repeat(jnp.exp(steps), extent[dim] // blocks).reshape((-1,) + (1,) * (len(extent) - dim - 1))

    level = one(*cuts[0])
    for cut in cuts[1:]:
        level = level * one(*cut)
    return level


def setup_inputs(seed: int = 0) -> dict:
    arg_keys = jax.random.split(jax.random.key(seed), 6)
    return {
        "image": draw_image(jax.random.fold_in(arg_keys[5], 71), 0),
        "inv_variance": jnp.clip(jnp.exp(math.log(4.0) - 2.7725887 * jax.random.uniform(arg_keys[1], (EPOCHS, ROWS, COLS), jnp.float32) ** levels(arg_keys[1], (EPOCHS, ROWS, COLS), ((0, 4), (1, 8)), -0.2, 0.2)), 0.25, 4.0).astype(jnp.bfloat16),
        "psf_rows": jnp.clip(jnp.exp(jax.random.uniform(arg_keys[2], (2 * PSF_HALF + 1,), jnp.float32, math.log(0.05), math.log(1.0))), 0.05, 1.0),
        "psf_cols": jnp.clip(jnp.exp(jax.random.uniform(arg_keys[3], (2 * PSF_HALF + 1,), jnp.float32, math.log(0.05), math.log(1.0))), 0.05, 1.0),
        "shift_num": draw_shift_num(jax.random.fold_in(arg_keys[5], 71), 0),
    }


def filter_epoch(pixels, weights_in, psf_rows, psf_cols):
    reach = PSF_HALF
    weighted = pixels * weights_in
    weighted_pad = jnp.pad(weighted, ((reach, reach), (reach, reach)))
    variance_pad = jnp.pad(weights_in, ((reach, reach), (reach, reach)))
    row_count = pixels.shape[0]
    col_count = pixels.shape[1]
    rows_psi = jnp.zeros((row_count, col_count + 2 * reach), jnp.float32)
    rows_phi = jnp.zeros((row_count, col_count + 2 * reach), jnp.float32)
    for offset in range(2 * reach + 1):
        rows_psi = rows_psi + psf_rows[offset] * weighted_pad[offset:offset + row_count, :]
        rows_phi = rows_phi + psf_rows[offset] * psf_rows[offset] * variance_pad[offset:offset + row_count, :]
    psi_map = jnp.zeros((row_count, col_count), jnp.float32)
    phi_map = jnp.zeros((row_count, col_count), jnp.float32)
    for offset in range(2 * reach + 1):
        psi_map = psi_map + psf_cols[offset] * rows_psi[:, offset:offset + col_count]
        phi_map = phi_map + psf_cols[offset] * psf_cols[offset] * rows_phi[:, offset:offset + col_count]
    return jnp.stack([psi_map, phi_map])

def shift_rows(padded, numerators, rim_width):
    row_count = padded.shape[2] - 2 * rim_width
    whole_rows = jnp.floor_divide(numerators, DEN)
    fraction = (numerators - whole_rows * DEN).astype(jnp.float32) / DEN
    start_rows = (rim_width - whole_rows - 1).astype(jnp.int32)

    def take_rows(one_block, start):
        return lax.dynamic_slice_in_dim(one_block, start, row_count + 1, axis=1)
    taken_rows = jax.vmap(take_rows)(padded, start_rows)
    fraction = fraction[:, None, None, None]
    return (1.0 - fraction) * taken_rows[:, :, 1:] + fraction * taken_rows[:, :, :-1]

def reference(image, inv_variance, psf_rows, psf_cols, shift_num):

    def one_epoch(pair):
        return filter_epoch(pair[0].astype(jnp.float32), pair[1].astype(jnp.float32), psf_rows, psf_cols)
    stacks = lax.map(one_epoch, jnp.stack([image, inv_variance], axis=1))
    row_count = stacks.shape[2]
    col_count = stacks.shape[3]
    for level_index in range(LEVELS):
        half_span = 2 ** level_index
        groups = EPOCHS // (2 * half_span)
        rim_width = VMAX * half_span + 1
        paired = stacks.reshape(groups, 2, half_span, 2, row_count, col_count)
        lower_half = paired[:, 0].reshape(groups * half_span, 2, row_count, col_count)
        upper_half = paired[:, 1].reshape(groups * half_span, 2, row_count, col_count)
        numerators = shift_num[level_index].reshape(groups, 2, half_span)
        padded = jnp.pad(upper_half, ((0, 0), (0, 0), (rim_width, rim_width), (0, 0)))
        new_lower = lower_half + shift_rows(padded, numerators[:, 0].reshape(-1), rim_width)
        new_upper = lower_half + shift_rows(padded, numerators[:, 1].reshape(-1), rim_width)
        stacks = jnp.stack([new_lower.reshape(groups, half_span, 2, row_count, col_count), new_upper.reshape(groups, half_span, 2, row_count, col_count)], axis=1)
        stacks = stacks.reshape(EPOCHS, 2, row_count, col_count)
    likelihood = stacks[:, 0] / jnp.sqrt(stacks[:, 1])
    peak_value = lax.optimization_barrier(jnp.max(likelihood, axis=0))
    return peak_value + jnp.log(lax.optimization_barrier(jnp.sum(jnp.exp(likelihood - peak_value[None]), axis=0)))
```

```python
import functools

import jax
import jax.numpy as jnp
from jax import lax
from jax.experimental import pallas as pl
from jax.experimental.pallas import tpu as pltpu
from jax.sharding import PartitionSpec as P

LEVELS = 4
PSF_HALF = 4
DEN = 4
VMAX = 2
LANES = 128
SUB = 8
BSUB = 16
MESH = pl.DeviceIdType.MESH


def flip(index, mask, size):
    result, bit = 0, 1
    while bit < size:
        digit = lax.rem(lax.div(index, bit), 2)
        result = result + bit * ((1 - digit) if mask & bit else digit)
        bit *= 2
    return result


def round_up(value, step):
    return (value + step - 1) // step * step


def halo_of(epoch):
    return round_up(VMAX * epoch + PSF_HALF, BSUB)


def classes_of(epochs):
    found = {}
    for e in range(epochs):
        first, count = found.get(halo_of(e), (e, 0))
        found[halo_of(e)] = (first, count + 1)
    return found


def runs_of(g, ep_local):
    runs = []
    for e in range(g * ep_local, (g + 1) * ep_local):
        if runs and runs[-1][0] == halo_of(e):
            runs[-1] = (runs[-1][0], runs[-1][1], runs[-1][2] + 1)
        else:
            runs.append((halo_of(e), e, 1))
    return runs


def plan_of(g, ep_local, row_count):
    blocks, used, left = [], [], []
    for e in range(ep_local):
        h = halo_of(g * ep_local + e)
        size = row_count + 2 * h
        first = min(size, LANES)
        blocks.append((e, len(used), 0, -h, first))
        used.append(first)
        if size > first:
            left.append((e, first - h, size - first))
    for e, row, size in left:
        at = next((t for t, u in enumerate(used) if u + size <= LANES), None)
        if at is None:
            at = len(used)
            used.append(0)
        blocks.append((e, at, used[at], row, size))
        used[at] += size
    return blocks, used


SEND_ORDER = "3120"


def send_order(n):
    if n == len(SEND_ORDER):
        return [int(c) for c in SEND_ORDER]
    return list(range(n - 1, 0, -1)) + [0]


def kernel(
    n, sky, image_hbm, variance_hbm, psf_rows, psf_cols, shift_num, out,
    image, variance, outgoing, pieces, bands, toeplitz, mid, *rest,
):
    ep_local, row_count = image.shape[0], image.shape[1]
    epochs = n * ep_local
    tiles = image.shape[2] // n // LANES
    reach = PSF_HALF
    local_levels = ep_local.bit_length() - 1
    classes = classes_of(epochs)
    runs = [runs_of(g, ep_local) for g in range(n)]
    plans = [plan_of(g, ep_local, row_count) for g in range(n)]
    rest = list(rest)
    above = {h: rest.pop(0) for h in classes}
    below = {h: rest.pop(0) for h in classes}
    matrices = [rest.pop(0) for _ in range(n)]
    wide = [rest.pop(0) for _ in range(LEVELS - local_levels)]
    in_sem, send_sem, recv_sem, down_send, down_recv, up_send, up_recv = rest
    class_at = {h: i for i, h in enumerate(classes)}
    run_at = {}
    for g in range(n):
        for run in runs[g]:
            run_at[run] = len(run_at)

    me = lax.axis_index("epoch")
    row_dev = lax.axis_index("sky")
    has_above = row_dev > 0
    has_below = row_dev < sky - 1
    groups = [flip(me, d, n) for d in range(n)]

    loads = [
        pltpu.make_async_copy(image_hbm, image, in_sem.at[0]),
        pltpu.make_async_copy(variance_hbm, variance, in_sem.at[1]),
    ]
    for load in loads:
        load.start()

    barrier = pltpu.get_barrier_semaphore()
    for d in range(1, n):
        pl.semaphore_signal(barrier, inc=1, device_id=(groups[d], row_dev), device_id_type=MESH)

    @pl.when(has_above)
    def _():
        pl.semaphore_signal(barrier, inc=1, device_id=(me, row_dev - 1), device_id_type=MESH)

    @pl.when(has_below)
    def _():
        pl.semaphore_signal(barrier, inc=1, device_id=(me, row_dev + 1), device_id_type=MESH)

    def make_bands():
        source = lax.broadcasted_iota(jnp.int32, (2 * LANES, LANES), 0)
        column = lax.broadcasted_iota(jnp.int32, (2 * LANES, LANES), 1)
        at = jnp.where(source < LANES + LANES // 2, source, source - 2 * LANES)
        tap = at - column + reach
        for m in range(2):
            band = jnp.zeros((2 * LANES, LANES), jnp.float32)
            for b in range(2 * reach + 1):
                weight = psf_cols[b] if m == 0 else psf_cols[b] * psf_cols[b]
                band = jnp.where(tap == b, weight, band)
            high = band.astype(jnp.bfloat16)
            bands[m, :, :LANES] = high
            bands[m, :, LANES:] = (band - high.astype(jnp.float32)).astype(jnp.bfloat16)

    lane = lax.broadcasted_iota(jnp.int32, (ep_local * row_count, LANES), 1)

    def filter_cols(p, tile, dest):
        here = p * tiles + tile
        flat = (ep_local * row_count, LANES)

        def take(ref, t):
            at = pl.multiple_of(t * LANES, LANES)
            return ref[:, :, pl.ds(at, LANES)].astype(jnp.float32).reshape(flat)

        def both(t, keep):
            v = take(variance, t)
            if keep is not None:
                v = v * keep
            return take(image, t) * v, v

        total = n * tiles
        left_on = jnp.where(here > 0, 1.0, 0.0).astype(jnp.float32)
        right_on = jnp.where(here < total - 1, 1.0, 0.0).astype(jnp.float32)
        left = both(jnp.maximum(here - 1, 0), left_on)
        centre = both(here, None)
        right = both(jnp.minimum(here + 1, total - 1), right_on)
        for m in range(2):
            edge = jnp.where(lane < LANES // 2, right[m], left[m])
            x = jnp.concatenate([centre[m], edge], axis=1)
            high = x.astype(jnp.bfloat16)
            y = jnp.dot(high, bands[m], preferred_element_type=jnp.float32)
            y = y[:, :LANES] + y[:, LANES:]
            if m == 0:
                low = (x - high.astype(jnp.float32)).astype(jnp.bfloat16)
                y = y + jnp.dot(low, bands[m, :, :LANES], preferred_element_type=jnp.float32)
            dest[:, m] = y.reshape(ep_local, row_count, LANES).astype(jnp.bfloat16)

    def piece_out(d, tile):
        return pltpu.make_async_remote_copy(
            src_ref=outgoing.at[d - 1, tile], dst_ref=pieces.at[me, tile],
            send_sem=send_sem.at[0], recv_sem=recv_sem.at[me, tile],
            device_id=(groups[d], row_dev), device_id_type=MESH,
        )

    def piece_in(d, tile):
        return pltpu.make_async_remote_copy(
            src_ref=outgoing.at[d - 1, tile], dst_ref=pieces.at[groups[d], tile],
            send_sem=send_sem.at[0], recv_sem=recv_sem.at[groups[d], tile],
            device_id=(groups[d], row_dev), device_id_type=MESH,
        )

    def halo_copy(down, run, tile):
        h, first, count = run
        g = first // ep_local
        e = first - g * ep_local
        at = first - classes[h][0]
        rows = pl.ds(row_count - h, h) if down else pl.ds(0, h)
        return pltpu.make_async_remote_copy(
            src_ref=pieces.at[g, tile, pl.ds(e, count), :, rows, :],
            dst_ref=(above if down else below)[h].at[tile, pl.ds(at, count)],
            send_sem=(down_send if down else up_send).at[class_at[h]],
            recv_sem=(down_recv if down else up_recv).at[run_at[run], tile],
            device_id=(me, row_dev + 1 if down else row_dev - 1), device_id_type=MESH,
        )

    def forward(d, tile):
        for g in range(n):
            @pl.when(groups[d] == g)
            def _():
                @pl.when(has_below)
                def _():
                    for run in runs[g]:
                        halo_copy(True, run, tile).start()

                @pl.when(has_above)
                def _():
                    for run in runs[g]:
                        halo_copy(False, run, tile).start()

    def wait_halo(g, tile):
        @pl.when(has_above)
        def _():
            for run in runs[g]:
                halo_copy(True, run, tile).wait_recv()

        @pl.when(has_below)
        def _():
            for run in runs[g]:
                halo_copy(False, run, tile).wait_recv()

    def clear_edges():
        for edge, refs in ((has_above, above), (has_below, below)):
            @pl.when(jnp.logical_not(edge))
            def _():
                for h, ref in refs.items():
                    for tile in range(tiles):
                        ref[tile] = jnp.zeros(ref.shape[1:], ref.dtype)

    first_row = jnp.where(has_above, -row_count, 0)
    end_row = jnp.where(has_below, 2 * row_count, row_count)

    def in_sky(row, size=BSUB):
        rows = lax.broadcasted_iota(jnp.int32, (size, LANES), 0) + row
        return jnp.logical_and(rows >= first_row, rows < end_row)

    def shift_of(level, index):
        number = shift_num[level, index]
        big = 2 * VMAX * 2**LEVELS
        whole = lax.div(number + DEN * big, DEN) - big
        left = number - whole * DEN
        fraction = left.astype(jnp.float32) / DEN
        return whole, whole + jnp.where(left > 0, 1, 0), fraction

    kinds = {}
    for blocks, _ in plans:
        for e, t, lane0, row0, size in blocks:
            key = (row0 - lane0, lane0 if lane0 else 0, bool(lane0))
            kinds.setdefault(key, len(kinds))

    def make_toeplitz():
        w = [psf_rows[b] for b in range(2 * reach + 1)]
        squares = [s * s for s in w]
        column = lax.broadcasted_iota(jnp.int32, (BSUB, LANES), 1)
        line = lax.broadcasted_iota(jnp.int32, (BSUB, LANES), 0)

        def body(b, carry):
            row = b * BSUB - row_count
            to = pl.multiple_of(b * BSUB, BSUB)
            keep = in_sky(row)
            for (offset, lane0, extra), at in kinds.items():
                tap = column - line - row + (offset + reach)
                ok = jnp.logical_and(keep, column >= lane0) if extra else keep
                tap = jnp.where(ok, tap, -1)
                for m, weights in enumerate((w, squares)):
                    value = jnp.zeros((BSUB, LANES), jnp.float32)
                    for a, weight in enumerate(weights):
                        value = jnp.where(tap == a, weight, value)
                    toeplitz[m, at, pl.ds(to, BSUB), :] = value
            return carry

        lax.fori_loop(0, 3 * row_count // BSUB, body, 0)

    def pad_of(g):
        return round_up(VMAX * g * ep_local, SUB)

    def mix(load, at, shift):
        near, far, fraction = shift
        return (1.0 - fraction) * load(at - near) + fraction * load(at - far)

    def make_matrix(g):
        base = g * ep_local
        blocks, used = plans[g]
        depth = len(used) * LANES

        def plane(ref, index):
            return lambda m: lambda at: ref[m, index, pl.ds(at, BSUB), :]

        state = []
        for e in range(ep_local):
            mine = {}
            for b, (epoch, t, lane0, row0, size) in enumerate(blocks):
                if epoch == e:
                    kind = kinds[(row0 - lane0, lane0, bool(lane0))]
                    mine[b] = (("toeplitz", kind), plane(toeplitz, kind))
            state.append(mine)
        planes = 0
        for level in range(local_levels - 1):
            half = 2**level
            made, following = [], [None] * ep_local
            for j in range(ep_local):
                if j & half:
                    continue
                for i in (j, j + half):
                    following[i] = dict(state[j])
                    for b, (_, source) in state[j + half].items():
                        made.append((planes, source, shift_of(level, base + i)))
                        following[i][b] = (("mid", planes), plane(mid, planes))
                        planes += 1
            pad = max(
                round_up(VMAX * (base + (j - j % (2 * half))), SUB) for j in range(ep_local)
            )

            def body(b, carry):
                row = b * BSUB - pad
                at = pl.multiple_of(row_count + row, SUB)
                keep = in_sky(row)
                for to, source, shift in made:
                    for m in range(2):
                        value = mix(source(m), at, shift)
                        mid[m, to, pl.ds(at, BSUB), :] = jnp.where(keep, value, 0.0)
                return carry

            lax.fori_loop(0, (row_count + 2 * pad) // BSUB, body, 0)
            state = following

        level = local_levels - 1
        half = 2**level
        pad = pad_of(g)
        size = row_count + 2 * pad
        entries = {}
        for j in range(half):
            for i in (j, j + half):
                for t in range(len(used)):
                    key = tuple(
                        (b, name, None) for b, (name, _) in state[j].items() if blocks[b][1] == t
                    ) + tuple(
                        (b, name, i) for b, (name, _) in state[j + half].items() if blocks[b][1] == t
                    )
                    entries.setdefault((t, key), []).append(i)
        sources = {name: source for mine in state for name, source in mine.values()}
        shifts = [shift_of(level, base + i) for i in range(ep_local)]
        ref = matrices[g]

        def body(b, carry):
            row = b * BSUB - pad
            at = pl.multiple_of(row_count + row, SUB)
            keep = in_sky(row)
            for (t, key), places in entries.items():
                for m in range(2):
                    value = None
                    for _, name, i in key:
                        load = sources[name](m)
                        part = load(at) if i is None else mix(load, at, shifts[i])
                        if i is not None:
                            part = jnp.where(keep, part, 0.0)
                        value = part if value is None else value + part
                    high = value.astype(jnp.bfloat16)
                    low = (value - high.astype(jnp.float32)).astype(jnp.bfloat16)
                    for i in places:
                        to = pl.multiple_of(i * size + b * BSUB, BSUB)
                        ref[m, pl.ds(to, BSUB), t * LANES:(t + 1) * LANES] = high
                        ref[m, pl.ds(to, BSUB), depth + t * LANES:depth + (t + 1) * LANES] = low
            return carry

        lax.fori_loop(0, size // BSUB, body, 0)

    def gather_rows(g, tile, m):
        blocks, used = plans[g]
        parts = []
        for t, filled in enumerate(used):
            for e, at, lane0, row0, size in sorted(blocks, key=lambda b: b[2]):
                if at != t:
                    continue
                epoch = g * ep_local + e
                h = halo_of(epoch)
                index = epoch - classes[h][0]
                row, end = row0, row0 + size
                if row < 0:
                    parts.append(above[h][tile, index, m, row + h:min(end, 0) + h, :])
                    row = min(end, 0)
                if row < min(end, row_count):
                    parts.append(pieces[g, tile, e, m, row:min(end, row_count), :])
                    row = min(end, row_count)
                if row < end:
                    parts.append(below[h][tile, index, m, row - row_count:end - row_count, :])
            if filled < LANES:
                parts.append(jnp.zeros((LANES - filled, LANES), jnp.bfloat16))
        return jnp.concatenate(parts, axis=0)

    def stack_group(g, tile):
        pad = pad_of(g)
        size = row_count + 2 * pad
        for m in range(2):
            x = gather_rows(g, tile, m)
            x = jnp.concatenate([x, x], axis=0)
            y = jnp.dot(matrices[g][m], x, preferred_element_type=jnp.float32)
            for i in range(ep_local):
                wide[0][g * ep_local + i, m, row_count - pad:row_count + row_count + pad, :] = (
                    y[i * size:(i + 1) * size]
                )

    keep_above = jnp.where(has_above, 1.0, 0.0).astype(jnp.float32)
    keep_below = jnp.where(has_below, 1.0, 0.0).astype(jnp.float32)

    def level_pass(level, src, dest, first):
        half = 2**level
        pad = round_up(VMAX * first, SUB)
        for j in range(first, first + half):
            outs = [(i, shift_of(level, i)) for i in (j, j + half)]
            for row in range(-pad, row_count + pad, SUB):
                at = row_count + row
                for m in range(2):
                    lower = src[j, m, at:at + SUB, :]
                    for i, (near, far, fraction) in outs:
                        x = src[j + half, m, pl.ds(at - near, SUB), :]
                        y = src[j + half, m, pl.ds(at - far, SUB), :]
                        value = lower + ((1.0 - fraction) * x + fraction * y)
                        if row < 0:
                            value = value * keep_above
                        if row >= row_count:
                            value = value * keep_below
                        dest[i, m, at:at + SUB, :] = value

    def finish(tile):
        for level in range(local_levels, LEVELS - 1):
            for first in range(0, epochs, 2 ** (level + 1)):
                level_pass(level, wide[level - local_levels], wide[level - local_levels + 1], first)
        final = wide[LEVELS - 1 - local_levels]
        half = epochs // 2
        shifts = [shift_of(LEVELS - 1, i) for i in range(epochs)]

        def body(b, carry):
            at = pl.multiple_of(row_count + b * SUB, SUB)
            likelihood = [None] * epochs
            for j in range(half):
                lower = [final[j, m, pl.ds(at, SUB), :] for m in range(2)]
                for index in (j, j + half):
                    near, far, fraction = shifts[index]
                    maps = []
                    for m in range(2):
                        x = final[j + half, m, pl.ds(at - near, SUB), :]
                        y = final[j + half, m, pl.ds(at - far, SUB), :]
                        maps.append(lower[m] + ((1.0 - fraction) * x + fraction * y))
                    likelihood[index] = maps[0] * lax.rsqrt(maps[1])
            peak = functools.reduce(jnp.maximum, likelihood)
            total = functools.reduce(jnp.add, [jnp.exp(x - peak) for x in likelihood])
            to = pl.multiple_of(b * SUB, SUB)
            out[pl.ds(to, SUB), tile * LANES:(tile + 1) * LANES] = peak + jnp.log(total)
            return carry

        lax.fori_loop(0, row_count // SUB, body, 0)

    make_bands()
    for load in loads:
        load.wait()
    order = send_order(n)
    for tile in range(tiles):
        for d in order:
            filter_cols(groups[d], tile, outgoing.at[d - 1, tile] if d else pieces.at[me, tile])
            if tile == 0 and d == order[0]:
                near = jnp.where(has_above, 1, 0) + jnp.where(has_below, 1, 0)
                pl.semaphore_wait(barrier, n - 1 + near)
            if d:
                piece_out(d, tile).start()
            else:
                forward(0, tile)

    clear_edges()
    make_toeplitz()
    for g in range(n):
        make_matrix(g)

    def process(tile):
        for g in range(n):
            wait_halo(g, tile)
            stack_group(g, tile)
        finish(tile)

    for tile in range(tiles):
        for d in order:
            if d:
                piece_in(d, tile).wait_recv()
                forward(d, tile)
        if tile:
            process(tile - 1)
    process(tiles - 1)

    pltpu.make_async_remote_copy(
        src_ref=outgoing, dst_ref=pieces.at[pl.ds(0, n - 1)], send_sem=send_sem.at[0],
        recv_sem=recv_sem.at[0, 0], device_id=(groups[1], row_dev), device_id_type=MESH,
    ).wait_send()
    for edge, refs, sem, step in ((has_below, above, down_send, 1), (has_above, below, up_send, -1)):
        @pl.when(edge)
        def _():
            for h, ref in refs.items():
                pltpu.make_async_remote_copy(
                    src_ref=ref, dst_ref=ref, send_sem=sem.at[class_at[h]],
                    recv_sem=down_recv.at[0, 0], device_id=(me, row_dev + step),
                    device_id_type=MESH,
                ).wait_send()


def on_device(n, sky, image, inv_variance, psf_rows, psf_cols, shift_num):
    ep_local, row_count, cols = image.shape
    tiles = cols // n // LANES
    epochs = n * ep_local
    local_levels = ep_local.bit_length() - 1
    piece = (tiles, ep_local, 2, row_count, LANES)
    classes = classes_of(epochs)
    plans = [plan_of(g, ep_local, row_count) for g in range(n)]
    kinds = {(b[3] - b[2], b[2]) for blocks, _ in plans for b in blocks}
    run_count = sum(len(runs_of(g, ep_local)) for g in range(n))
    halos = [
        pltpu.VMEM((tiles, count, 2, h, LANES), jnp.bfloat16) for h, (_, count) in classes.items()
    ]
    matrices = []
    for g in range(n):
        size = row_count + 2 * round_up(VMAX * g * ep_local, SUB)
        depth = 2 * LANES * len(plans[g][1])
        matrices.append(pltpu.VMEM((2, ep_local * size, depth), jnp.bfloat16))
    most = max(len(blocks) for blocks, _ in plans)

    any_space = pl.BlockSpec(memory_space=pl.ANY)
    vmem = pl.BlockSpec(memory_space=pltpu.VMEM)
    smem = pl.BlockSpec(memory_space=pltpu.SMEM)
    return pl.pallas_call(
        functools.partial(kernel, n, sky),
        out_shape=jax.ShapeDtypeStruct((row_count, cols // n), jnp.float32),
        in_specs=[any_space, any_space, smem, smem, smem],
        out_specs=vmem,
        scratch_shapes=[
            pltpu.VMEM(image.shape, jnp.bfloat16),
            pltpu.VMEM(image.shape, jnp.bfloat16),
            pltpu.VMEM((n - 1,) + piece, jnp.bfloat16),
            pltpu.VMEM((n,) + piece, jnp.bfloat16),
            pltpu.VMEM((2, 2 * LANES, 2 * LANES), jnp.bfloat16),
            pltpu.VMEM((2, len(kinds), 3 * row_count, LANES), jnp.float32),
            pltpu.VMEM((2, max(1, local_levels * most), 3 * row_count, LANES), jnp.float32),
        ]
        + halos + halos + matrices
        + [
            pltpu.VMEM((epochs, 2, 3 * row_count, LANES), jnp.float32)
            for _ in range(LEVELS - local_levels)
        ]
        + [
            pltpu.SemaphoreType.DMA((2,)),
            pltpu.SemaphoreType.DMA((1,)),
            pltpu.SemaphoreType.DMA((n, tiles)),
            pltpu.SemaphoreType.DMA((len(classes),)),
            pltpu.SemaphoreType.DMA((run_count, tiles)),
            pltpu.SemaphoreType.DMA((len(classes),)),
            pltpu.SemaphoreType.DMA((run_count, tiles)),
        ],
        compiler_params=pltpu.CompilerParams(
            collective_id=0, has_side_effects=True, vmem_limit_bytes=60 * 1024 * 1024
        ),
    )(image, inv_variance, psf_rows, psf_cols, shift_num)


def solution(mesh):
    body = functools.partial(on_device, mesh.shape["epoch"], mesh.shape["sky"])
    return jax.shard_map(
        body,
        mesh=mesh,
        in_specs=(P("epoch", "sky", None), P("epoch", "sky", None), P(), P(), P()),
        out_specs=P("sky", "epoch"),
        check_vma=False,
    )
```

```python
import functools

import jax
import jax.numpy as jnp
from jax import lax
from jax.experimental import pallas as pl
from jax.experimental.pallas import tpu as pltpu
from jax.sharding import PartitionSpec as P

LEVELS = 4
PSF_HALF = 4
DEN = 4
VMAX = 2
LANES = 128
SUB = 8
BSUB = 16
MESH = pl.DeviceIdType.MESH


def flip(index, mask, size):
    result, bit = 0, 1
    while bit < size:
        digit = lax.rem(lax.div(index, bit), 2)
        result = result + bit * ((1 - digit) if mask & bit else digit)
        bit *= 2
    return result


def round_up(value, step):
    return (value + step - 1) // step * step


def halo_of(epoch):
    return round_up(VMAX * epoch + PSF_HALF, BSUB)


def classes_of(epochs):
    found = {}
    for e in range(epochs):
        first, count = found.get(halo_of(e), (e, 0))
        found[halo_of(e)] = (first, count + 1)
    return found


def runs_of(start, count):
    runs = []
    for e in range(start, start + count):
        if runs and runs[-1][0] == halo_of(e):
            runs[-1] = (runs[-1][0], runs[-1][1], runs[-1][2] + 1)
        else:
            runs.append((halo_of(e), e, 1))
    return runs


def plan_of(g, ep_local, row_count):
    blocks, used, left = [], [], []
    for e in range(ep_local):
        h = halo_of(g * ep_local + e)
        size = row_count + 2 * h
        first = min(size, LANES)
        blocks.append((e, len(used), 0, -h, first))
        used.append(first)
        if size > first:
            left.append((e, first - h, size - first))
    for e, row, size in left:
        at = next((t for t, u in enumerate(used) if u + size <= LANES), None)
        if at is None:
            at = len(used)
            used.append(0)
        blocks.append((e, at, used[at], row, size))
        used[at] += size
    return blocks, used


def send_order(n):
    return sorted(range(1, n), key=lambda d: (-bin(d).count("1"), d)) + [0]


def parts_of(tile, tiles, ep_local):
    if tile < tiles - 1 or ep_local == 1:
        return [(0, ep_local, tile)]
    half = ep_local // 2
    return [(0, half, tile), (half, ep_local - half, tiles)]


def kernel(
    n, sky, image_hbm, variance_hbm, psf_rows_hbm, psf_cols_hbm, shift_hbm, out,
    image, variance, psf_rows, psf_cols, shift_num,
    outgoing, pieces, bands, toeplitz, mid, counted, *rest,
):
    ep_local, row_count = image.shape[0], image.shape[1]
    epochs = n * ep_local
    tiles = image.shape[2] // n // LANES
    reach = PSF_HALF
    local_levels = ep_local.bit_length() - 1
    classes = classes_of(epochs)
    plans = [plan_of(g, ep_local, row_count) for g in range(n)]
    rest = list(rest)
    above = {h: rest.pop(0) for h in classes}
    below = {h: rest.pop(0) for h in classes}
    matrices = [rest.pop(0) for _ in range(n)]
    wide = [rest.pop(0) for _ in range(LEVELS - local_levels)]
    in_sem, send_sem, recv_sem, halo_recv = rest

    me = lax.axis_index("epoch")
    row_dev = lax.axis_index("sky")
    has_above = row_dev > 0
    has_below = row_dev < sky - 1
    groups = [flip(me, d, n) for d in range(n)]

    barrier = pltpu.get_barrier_semaphore()
    for d in range(1, n):
        pl.semaphore_signal(barrier, inc=1, device_id=(groups[d], row_dev), device_id_type=MESH)

    @pl.when(has_above)
    def _():
        pl.semaphore_signal(barrier, inc=1, device_id=(me, row_dev - 1), device_id_type=MESH)

    @pl.when(has_below)
    def _():
        pl.semaphore_signal(barrier, inc=1, device_id=(me, row_dev + 1), device_id_type=MESH)

    whole = (
        (psf_cols_hbm, psf_cols), (image_hbm, image), (variance_hbm, variance),
        (psf_rows_hbm, psf_rows), (shift_hbm, shift_num),
    )
    loads = [pltpu.make_async_copy(a, b, in_sem.at[i]) for i, (a, b) in enumerate(whole)]
    for load in loads:
        load.start()

    def make_bands():
        source = lax.broadcasted_iota(jnp.int32, (2 * LANES, LANES), 0)
        column = lax.broadcasted_iota(jnp.int32, (2 * LANES, LANES), 1)
        at = jnp.where(source < LANES + LANES // 2, source, source - 2 * LANES)
        tap = at - column + reach
        for m in range(2):
            band = jnp.zeros((2 * LANES, LANES), jnp.float32)
            for b in range(2 * reach + 1):
                weight = psf_cols[b] if m == 0 else psf_cols[b] * psf_cols[b]
                band = jnp.where(tap == b, weight, band)
            high = band.astype(jnp.bfloat16)
            bands[m, :, :LANES] = high
            bands[m, :, LANES:] = (band - high.astype(jnp.float32)).astype(jnp.bfloat16)

    lane = lax.broadcasted_iota(jnp.int32, (ep_local * row_count, LANES), 1)

    def filter_cols(p, tile, dest):
        here = p * tiles + tile
        flat = (ep_local * row_count, LANES)

        def take(ref, t):
            at = pl.multiple_of(t * LANES, LANES)
            return ref[:, :, pl.ds(at, LANES)].astype(jnp.float32).reshape(flat)

        def both(t, keep):
            v = take(variance, t)
            if keep is not None:
                v = v * keep
            return take(image, t) * v, v

        total = n * tiles
        left_on = jnp.where(here > 0, 1.0, 0.0).astype(jnp.float32)
        right_on = jnp.where(here < total - 1, 1.0, 0.0).astype(jnp.float32)
        left = both(jnp.maximum(here - 1, 0), left_on)
        centre = both(here, None)
        right = both(jnp.minimum(here + 1, total - 1), right_on)
        for m in range(2):
            edge = jnp.where(lane < LANES // 2, right[m], left[m])
            x = jnp.concatenate([centre[m], edge], axis=1)
            high = x.astype(jnp.bfloat16)
            y = jnp.dot(high, bands[m], preferred_element_type=jnp.float32)
            y = y[:, :LANES] + y[:, LANES:]
            if m == 0:
                low = (x - high.astype(jnp.float32)).astype(jnp.bfloat16)
                y = y + jnp.dot(low, bands[m, :, :LANES], preferred_element_type=jnp.float32)
            dest[:, m] = y.reshape(ep_local, row_count, LANES).astype(jnp.bfloat16)

    def piece_copy(d, tile, part, group):
        first, count, slot = part
        epochs_of = pl.ds(first, count)
        return pltpu.make_async_remote_copy(
            src_ref=outgoing.at[d - 1, tile, epochs_of], dst_ref=pieces.at[group, tile, epochs_of],
            send_sem=send_sem.at[0], recv_sem=recv_sem.at[d - 1, slot],
            device_id=(groups[d], row_dev), device_id_type=MESH,
        )

    def halo_copy(down, run, tile, slot):
        h, start, count = run
        g = start // ep_local
        at = start - classes[h][0]
        rows = pl.ds(row_count - h, h) if down else pl.ds(0, h)
        return pltpu.make_async_remote_copy(
            src_ref=pieces.at[g, tile, pl.ds(start - g * ep_local, count), :, rows, :],
            dst_ref=(above if down else below)[h].at[tile, pl.ds(at, count)],
            send_sem=send_sem.at[1 if down else 2], recv_sem=halo_recv.at[g, slot],
            device_id=(me, row_dev + 1 if down else row_dev - 1), device_id_type=MESH,
        )

    def each_group(d, use):
        for g in range(n):
            pl.when(groups[d] == g)(functools.partial(use, g))

    def forward(d, tile, part):
        first, count, slot = part

        def use(g):
            runs = runs_of(g * ep_local + first, count)

            @pl.when(has_below)
            def _():
                for run in runs:
                    halo_copy(True, run, tile, slot).start()

            @pl.when(has_above)
            def _():
                for run in runs:
                    halo_copy(False, run, tile, slot).start()

        each_group(d, use)

    def counting(rows, send, recv):
        return pltpu.make_async_remote_copy(
            src_ref=counted.at[pl.ds(0, rows)], dst_ref=counted.at[pl.ds(0, rows)],
            send_sem=send, recv_sem=recv, device_id=(groups[1], row_dev), device_id_type=MESH,
        )

    def wait_halo(g, part):
        first, count, slot = part
        rows = sum(2 * h * c for h, _, c in runs_of(g * ep_local + first, count))
        sem = halo_recv.at[g, slot]

        @pl.when(jnp.logical_and(has_above, has_below))
        def _():
            counting(2 * rows, send_sem.at[0], sem).wait_recv()

        @pl.when(has_above != has_below)
        def _():
            counting(rows, send_sem.at[0], sem).wait_recv()

    def clear_edges():
        for edge, refs in ((has_above, above), (has_below, below)):
            @pl.when(jnp.logical_not(edge))
            def _():
                for h, ref in refs.items():
                    for tile in range(tiles):
                        ref[tile] = jnp.zeros(ref.shape[1:], ref.dtype)

    first_row = jnp.where(has_above, -row_count, 0)
    end_row = jnp.where(has_below, 2 * row_count, row_count)

    def in_sky(row, size=BSUB):
        rows = lax.broadcasted_iota(jnp.int32, (size, LANES), 0) + row
        return jnp.logical_and(rows >= first_row, rows < end_row)

    def shift_of(level, index):
        number = shift_num[level, index]
        big = 2 * VMAX * 2**LEVELS
        whole = lax.div(number + DEN * big, DEN) - big
        left = number - whole * DEN
        fraction = left.astype(jnp.float32) / DEN
        return whole, whole + jnp.where(left > 0, 1, 0), fraction

    kinds = {}
    for blocks, _ in plans:
        for e, t, lane0, row0, size in blocks:
            key = (row0 - lane0, lane0 if lane0 else 0, bool(lane0))
            kinds.setdefault(key, len(kinds))

    def make_toeplitz():
        w = [psf_rows[b] for b in range(2 * reach + 1)]
        squares = [s * s for s in w]
        column = lax.broadcasted_iota(jnp.int32, (BSUB, LANES), 1)
        line = lax.broadcasted_iota(jnp.int32, (BSUB, LANES), 0)

        def body(b, carry):
            row = b * BSUB - row_count
            to = pl.multiple_of(b * BSUB, BSUB)
            keep = in_sky(row)
            for (offset, lane0, extra), at in kinds.items():
                tap = column - line - row + (offset + reach)
                ok = jnp.logical_and(keep, column >= lane0) if extra else keep
                tap = jnp.where(ok, tap, -1)
                for m, weights in enumerate((w, squares)):
                    value = jnp.zeros((BSUB, LANES), jnp.float32)
                    for a, weight in enumerate(weights):
                        value = jnp.where(tap == a, weight, value)
                    toeplitz[m, at, pl.ds(to, BSUB), :] = value
            return carry

        lax.fori_loop(0, 3 * row_count // BSUB, body, 0)

    def pad_of(g):
        return round_up(VMAX * g * ep_local, SUB)

    def mix(load, at, shift):
        near, far, fraction = shift
        return (1.0 - fraction) * load(at - near) + fraction * load(at - far)

    def make_matrix(g):
        base = g * ep_local
        blocks, used = plans[g]
        depth = len(used) * LANES

        def plane(ref, index):
            return lambda m: lambda at: ref[m, index, pl.ds(at, BSUB), :]

        state = []
        for e in range(ep_local):
            mine = {}
            for b, (epoch, t, lane0, row0, size) in enumerate(blocks):
                if epoch == e:
                    kind = kinds[(row0 - lane0, lane0, bool(lane0))]
                    mine[b] = (("toeplitz", kind), plane(toeplitz, kind))
            state.append(mine)
        planes = 0
        for level in range(local_levels - 1):
            half = 2**level
            made, following = [], [None] * ep_local
            for j in range(ep_local):
                if j & half:
                    continue
                for i in (j, j + half):
                    following[i] = dict(state[j])
                    for b, (_, source) in state[j + half].items():
                        made.append((planes, source, shift_of(level, base + i)))
                        following[i][b] = (("mid", planes), plane(mid, planes))
                        planes += 1
            pad = max(
                round_up(VMAX * (base + (j - j % (2 * half))), SUB) for j in range(ep_local)
            )

            def body(b, carry):
                row = b * BSUB - pad
                at = pl.multiple_of(row_count + row, SUB)
                keep = in_sky(row)
                for to, source, shift in made:
                    for m in range(2):
                        value = mix(source(m), at, shift)
                        mid[m, to, pl.ds(at, BSUB), :] = jnp.where(keep, value, 0.0)
                return carry

            lax.fori_loop(0, (row_count + 2 * pad) // BSUB, body, 0)
            state = following

        level = local_levels - 1
        half = 2**level
        pad = pad_of(g)
        size = row_count + 2 * pad
        entries = {}
        for j in range(half):
            for i in (j, j + half):
                for t in range(len(used)):
                    key = tuple(
                        (b, name, None) for b, (name, _) in state[j].items() if blocks[b][1] == t
                    ) + tuple(
                        (b, name, i) for b, (name, _) in state[j + half].items() if blocks[b][1] == t
                    )
                    entries.setdefault((t, key), []).append(i)
        sources = {name: source for mine in state for name, source in mine.values()}
        shifts = [shift_of(level, base + i) for i in range(ep_local)]
        ref = matrices[g]

        def body(b, carry):
            row = b * BSUB - pad
            at = pl.multiple_of(row_count + row, SUB)
            keep = in_sky(row)
            for (t, key), places in entries.items():
                for m in range(2):
                    value = None
                    for _, name, i in key:
                        load = sources[name](m)
                        part = load(at) if i is None else mix(load, at, shifts[i])
                        if i is not None:
                            part = jnp.where(keep, part, 0.0)
                        value = part if value is None else value + part
                    high = value.astype(jnp.bfloat16)
                    low = (value - high.astype(jnp.float32)).astype(jnp.bfloat16)
                    for i in places:
                        to = pl.multiple_of(i * size + b * BSUB, BSUB)
                        ref[m, pl.ds(to, BSUB), t * LANES:(t + 1) * LANES] = high
                        ref[m, pl.ds(to, BSUB), depth + t * LANES:depth + (t + 1) * LANES] = low
            return carry

        lax.fori_loop(0, size // BSUB, body, 0)

    def gather_rows(g, tile, m):
        blocks, used = plans[g]
        parts = []
        for t, filled in enumerate(used):
            for e, at, lane0, row0, size in sorted(blocks, key=lambda b: b[2]):
                if at != t:
                    continue
                epoch = g * ep_local + e
                h = halo_of(epoch)
                index = epoch - classes[h][0]
                row, end = row0, row0 + size
                if row < 0:
                    parts.append(above[h][tile, index, m, row + h:min(end, 0) + h, :])
                    row = min(end, 0)
                if row < min(end, row_count):
                    parts.append(pieces[g, tile, e, m, row:min(end, row_count), :])
                    row = min(end, row_count)
                if row < end:
                    parts.append(below[h][tile, index, m, row - row_count:end - row_count, :])
            if filled < LANES:
                parts.append(jnp.zeros((LANES - filled, LANES), jnp.bfloat16))
        return jnp.concatenate(parts, axis=0)

    def stack_group(g, tile):
        pad = pad_of(g)
        size = row_count + 2 * pad
        for m in range(2):
            x = gather_rows(g, tile, m)
            x = jnp.concatenate([x, x], axis=0)
            y = jnp.dot(matrices[g][m], x, preferred_element_type=jnp.float32)
            for i in range(ep_local):
                wide[0][g * ep_local + i, m, row_count - pad:row_count + row_count + pad, :] = (
                    y[i * size:(i + 1) * size]
                )

    keep_above = jnp.where(has_above, 1.0, 0.0).astype(jnp.float32)
    keep_below = jnp.where(has_below, 1.0, 0.0).astype(jnp.float32)

    def level_pass(level, src, dest, first):
        half = 2**level
        pad = round_up(VMAX * first, SUB)
        for j in range(first, first + half):
            outs = [(i, shift_of(level, i)) for i in (j, j + half)]
            outs = [(i, row_count - near, row_count - far, f) for i, (near, far, f) in outs]
            for row in range(-pad, row_count + pad, SUB):
                at = row_count + row
                for m in range(2):
                    lower = src[j, m, at:at + SUB, :]
                    for i, near, far, fraction in outs:
                        x = src[j + half, m, pl.ds(near + row, SUB), :]
                        y = src[j + half, m, pl.ds(far + row, SUB), :]
                        value = lower + ((1.0 - fraction) * x + fraction * y)
                        if row < 0:
                            value = value * keep_above
                        if row >= row_count:
                            value = value * keep_below
                        dest[i, m, at:at + SUB, :] = value

    def finish(tile):
        for level in range(local_levels, LEVELS - 1):
            for first in range(0, epochs, 2 ** (level + 1)):
                level_pass(level, wide[level - local_levels], wide[level - local_levels + 1], first)
        final = wide[LEVELS - 1 - local_levels]
        half = epochs // 2
        shifts = [shift_of(LEVELS - 1, i) for i in range(epochs)]
        shifts = [(row_count - near, row_count - far, f) for near, far, f in shifts]

        for row in range(0, row_count, SUB):
            at = row_count + row
            likelihood = [None] * epochs
            for j in range(half):
                lower = [final[j, m, at:at + SUB, :] for m in range(2)]
                for index in (j, j + half):
                    near, far, fraction = shifts[index]
                    maps = []
                    for m in range(2):
                        x = final[j + half, m, pl.ds(near + row, SUB), :]
                        y = final[j + half, m, pl.ds(far + row, SUB), :]
                        maps.append(lower[m] + ((1.0 - fraction) * x + fraction * y))
                    likelihood[index] = maps[0] * lax.rsqrt(maps[1])
            peak = functools.reduce(jnp.maximum, likelihood)
            total = functools.reduce(jnp.add, [jnp.exp(x - peak) for x in likelihood])
            out[row:row + SUB, tile * LANES:(tile + 1) * LANES] = peak + jnp.log(total)

    loads[0].wait()
    make_bands()
    for load in loads[1:]:
        load.wait()
    order = send_order(n)
    for tile in range(tiles):
        for d in order:
            filter_cols(groups[d], tile, outgoing.at[d - 1, tile] if d else pieces.at[me, tile])
            if tile == 0 and d == order[0]:
                near = jnp.where(has_above, 1, 0) + jnp.where(has_below, 1, 0)
                pl.semaphore_wait(barrier, n - 1 + near)
            parts = parts_of(tile, tiles, ep_local)
            if d:
                piece_copy(d, tile, parts[0], me).start()
            else:
                for part in parts[1:]:
                    for other in order[:-1]:
                        piece_copy(other, tile, part, me).start()
                for part in parts:
                    forward(0, tile, part)

    clear_edges()
    make_toeplitz()
    for g in range(n):
        make_matrix(g)

    def stack_tile(g, tile):
        for part in parts_of(tile, tiles, ep_local):
            wait_halo(g, part)
        stack_group(g, tile)

    for tile in range(tiles):
        for part in parts_of(tile, tiles, ep_local):
            for d in order[:-1]:
                piece_copy(d, tile, part, groups[d]).wait_recv()
                forward(d, tile, part)
        if tile:
            for g in range(n):
                stack_tile(g, tile - 1)
            finish(tile - 1)
    for d in [0] + order[:-1]:
        each_group(d, functools.partial(stack_tile, tile=tiles - 1))
    finish(tiles - 1)

    pltpu.make_async_remote_copy(
        src_ref=outgoing, dst_ref=pieces.at[pl.ds(0, n - 1)], send_sem=send_sem.at[0],
        recv_sem=recv_sem.at[0, 0], device_id=(groups[1], row_dev), device_id_type=MESH,
    ).wait_send()
    for edge, sem in ((has_below, send_sem.at[1]), (has_above, send_sem.at[2])):
        @pl.when(edge)
        def _():
            counting(counted.shape[0], sem, recv_sem.at[0, 0]).wait_send()


def on_device(n, sky, image, inv_variance, psf_rows, psf_cols, shift_num):
    ep_local, row_count, cols = image.shape
    tiles = cols // n // LANES
    epochs = n * ep_local
    local_levels = ep_local.bit_length() - 1
    piece = (tiles, ep_local, 2, row_count, LANES)
    classes = classes_of(epochs)
    plans = [plan_of(g, ep_local, row_count) for g in range(n)]
    kinds = {(b[3] - b[2], b[2]) for blocks, _ in plans for b in blocks}
    halo_rows = sum(2 * tiles * halo_of(e) for e in range(epochs))
    halos = [
        pltpu.VMEM((tiles, count, 2, h, LANES), jnp.bfloat16) for h, (_, count) in classes.items()
    ]
    matrices = []
    for g in range(n):
        size = row_count + 2 * round_up(VMAX * g * ep_local, SUB)
        depth = 2 * LANES * len(plans[g][1])
        matrices.append(pltpu.VMEM((2, ep_local * size, depth), jnp.bfloat16))
    most = max(len(blocks) for blocks, _ in plans)

    any_space = pl.BlockSpec(memory_space=pl.ANY)
    vmem = pl.BlockSpec(memory_space=pltpu.VMEM)
    return pl.pallas_call(
        functools.partial(kernel, n, sky),
        out_shape=pltpu.VMEM((row_count, cols // n), jnp.float32),
        in_specs=[any_space] * 5,
        out_specs=vmem,
        scratch_shapes=[
            pltpu.VMEM(image.shape, jnp.bfloat16),
            pltpu.VMEM(image.shape, jnp.bfloat16),
            pltpu.SMEM(psf_rows.shape, jnp.float32),
            pltpu.SMEM(psf_cols.shape, jnp.float32),
            pltpu.SMEM(shift_num.shape, jnp.int32),
            pltpu.VMEM((n - 1,) + piece, jnp.bfloat16),
            pltpu.VMEM((n,) + piece, jnp.bfloat16),
            pltpu.VMEM((2, 2 * LANES, 2 * LANES), jnp.bfloat16),
            pltpu.VMEM((2, len(kinds), 3 * row_count, LANES), jnp.float32),
            pltpu.VMEM((2, max(1, local_levels * most), 3 * row_count, LANES), jnp.float32),
            pltpu.VMEM((halo_rows, LANES), jnp.bfloat16),
        ]
        + halos + halos + matrices
        + [
            pltpu.VMEM((epochs, 2, 3 * row_count, LANES), jnp.float32)
            for _ in range(LEVELS - local_levels)
        ]
        + [
            pltpu.SemaphoreType.DMA((5,)),
            pltpu.SemaphoreType.DMA((3,)),
            pltpu.SemaphoreType.DMA((n - 1, tiles + 1)),
            pltpu.SemaphoreType.DMA((n, tiles + 1)),
        ],
        compiler_params=pltpu.CompilerParams(
            collective_id=0, has_side_effects=True, vmem_limit_bytes=60 * 1024 * 1024
        ),
    )(image, inv_variance, psf_rows, psf_cols, shift_num)


def solution(mesh):
    body = functools.partial(on_device, mesh.shape["epoch"], mesh.shape["sky"])
    return jax.shard_map(
        body,
        mesh=mesh,
        in_specs=(P("epoch", "sky", None), P("epoch", "sky", None), P(), P(), P()),
        out_specs=P("sky", "epoch"),
        check_vma=False,
    )
```

```python
import functools

import jax
import jax.numpy as jnp
from jax import lax
from jax.experimental import pallas as pl
from jax.experimental.pallas import tpu as pltpu
from jax.sharding import PartitionSpec as P

LEVELS = 4
PSF_HALF = 4
DEN = 4
VMAX = 2
LANES = 128
SUB = 8
BSUB = 16
FINAL = 16
HOLD = 1
MESH = pl.DeviceIdType.MESH


def flip(index, mask, size):
    result, bit = 0, 1
    while bit < size:
        digit = lax.rem(lax.div(index, bit), 2)
        result = result + bit * ((1 - digit) if mask & bit else digit)
        bit *= 2
    return result


def round_up(value, step):
    return (value + step - 1) // step * step


def halo_of(epoch):
    return round_up(VMAX * epoch + PSF_HALF, BSUB)


def classes_of(epochs):
    found = {}
    for e in range(epochs):
        first, count = found.get(halo_of(e), (e, 0))
        found[halo_of(e)] = (first, count + 1)
    return found


def runs_of(start, count):
    runs = []
    for e in range(start, start + count):
        if runs and runs[-1][0] == halo_of(e):
            runs[-1] = (runs[-1][0], runs[-1][1], runs[-1][2] + 1)
        else:
            runs.append((halo_of(e), e, 1))
    return runs


def plan_of(g, ep_local, row_count):
    blocks, used, left = [], [], []
    for e in range(ep_local):
        h = halo_of(g * ep_local + e)
        size = row_count + 2 * h
        first = min(size, LANES)
        blocks.append((e, len(used), 0, -h, first))
        used.append(first)
        if size > first:
            left.append((e, first - h, size - first))
    for e, row, size in left:
        at = next((t for t, u in enumerate(used) if u + size <= LANES), None)
        if at is None:
            at = len(used)
            used.append(0)
        blocks.append((e, at, used[at], row, size))
        used[at] += size
    return blocks, used


def send_order(n):
    return sorted(range(1, n), key=lambda d: (-bin(d).count("1"), d)) + [0]


def parts_of(tile, tiles, ep_local):
    if tile < tiles - 1 or ep_local == 1:
        return [(0, ep_local, tile)]
    half = ep_local // 2
    return [(0, half, tile), (half, ep_local - half, tiles)]


def kernel(
    n, sky, image_hbm, variance_hbm, psf_rows_hbm, psf_cols_hbm, shift_hbm, out,
    image, variance, psf_rows, psf_cols, shift_num,
    outgoing, pieces, bands, toeplitz, mid, counted, *rest,
):
    ep_local, row_count = image.shape[0], image.shape[1]
    epochs = n * ep_local
    tiles = image.shape[2] // n // LANES
    reach = PSF_HALF
    local_levels = ep_local.bit_length() - 1
    classes = classes_of(epochs)
    plans = [plan_of(g, ep_local, row_count) for g in range(n)]
    rest = list(rest)
    above = {h: rest.pop(0) for h in classes}
    below = {h: rest.pop(0) for h in classes}
    matrices = [rest.pop(0) for _ in range(n)]
    wide = [rest.pop(0) for _ in range(LEVELS - local_levels)]
    in_sem, send_sem, recv_sem, halo_recv = rest

    me = lax.axis_index("epoch")
    row_dev = lax.axis_index("sky")
    has_above = row_dev > 0
    has_below = row_dev < sky - 1
    groups = [flip(me, d, n) for d in range(n)]

    barrier = pltpu.get_barrier_semaphore()
    for d in range(1, n):
        pl.semaphore_signal(barrier, inc=1, device_id=(groups[d], row_dev), device_id_type=MESH)

    @pl.when(has_above)
    def _():
        pl.semaphore_signal(barrier, inc=1, device_id=(me, row_dev - 1), device_id_type=MESH)

    @pl.when(has_below)
    def _():
        pl.semaphore_signal(barrier, inc=1, device_id=(me, row_dev + 1), device_id_type=MESH)

    whole = (
        (psf_cols_hbm, psf_cols), (image_hbm, image), (variance_hbm, variance),
        (psf_rows_hbm, psf_rows), (shift_hbm, shift_num),
    )
    loads = [pltpu.make_async_copy(a, b, in_sem.at[i]) for i, (a, b) in enumerate(whole)]
    for load in loads:
        load.start()

    def make_bands():
        source = lax.broadcasted_iota(jnp.int32, (2 * LANES, LANES), 0)
        column = lax.broadcasted_iota(jnp.int32, (2 * LANES, LANES), 1)
        at = jnp.where(source < LANES + LANES // 2, source, source - 2 * LANES)
        tap = at - column + reach
        for m in range(2):
            band = jnp.zeros((2 * LANES, LANES), jnp.float32)
            for b in range(2 * reach + 1):
                weight = psf_cols[b] if m == 0 else psf_cols[b] * psf_cols[b]
                band = jnp.where(tap == b, weight, band)
            high = band.astype(jnp.bfloat16)
            bands[m, :, :LANES] = high
            bands[m, :, LANES:] = (band - high.astype(jnp.float32)).astype(jnp.bfloat16)

    lane = lax.broadcasted_iota(jnp.int32, (ep_local * row_count, LANES), 1)

    def filter_cols(p, tile, dest):
        here = p * tiles + tile
        flat = (ep_local * row_count, LANES)

        def take(ref, t):
            at = pl.multiple_of(t * LANES, LANES)
            return ref[:, :, pl.ds(at, LANES)].astype(jnp.float32).reshape(flat)

        def both(t, keep):
            v = take(variance, t)
            if keep is not None:
                v = v * keep
            return take(image, t) * v, v

        total = n * tiles
        left_on = jnp.where(here > 0, 1.0, 0.0).astype(jnp.float32)
        right_on = jnp.where(here < total - 1, 1.0, 0.0).astype(jnp.float32)
        left = both(jnp.maximum(here - 1, 0), left_on)
        centre = both(here, None)
        right = both(jnp.minimum(here + 1, total - 1), right_on)
        for m in range(2):
            edge = jnp.where(lane < LANES // 2, right[m], left[m])
            x = jnp.concatenate([centre[m], edge], axis=1)
            high = x.astype(jnp.bfloat16)
            y = jnp.dot(high, bands[m], preferred_element_type=jnp.float32)
            y = y[:, :LANES] + y[:, LANES:]
            if m == 0:
                low = (x - high.astype(jnp.float32)).astype(jnp.bfloat16)
                y = y + jnp.dot(low, bands[m, :, :LANES], preferred_element_type=jnp.float32)
            dest[:, m] = y.reshape(ep_local, row_count, LANES).astype(jnp.bfloat16)

    def piece_copy(d, tile, part, group):
        first, count, slot = part
        epochs_of = pl.ds(first, count)
        return pltpu.make_async_remote_copy(
            src_ref=outgoing.at[d - 1, tile, epochs_of], dst_ref=pieces.at[group, tile, epochs_of],
            send_sem=send_sem.at[0], recv_sem=recv_sem.at[d - 1, slot],
            device_id=(groups[d], row_dev), device_id_type=MESH,
        )

    def halo_copy(down, run, tile, slot):
        h, start, count = run
        g = start // ep_local
        at = start - classes[h][0]
        rows = pl.ds(row_count - h, h) if down else pl.ds(0, h)
        return pltpu.make_async_remote_copy(
            src_ref=pieces.at[g, tile, pl.ds(start - g * ep_local, count), :, rows, :],
            dst_ref=(above if down else below)[h].at[tile, pl.ds(at, count)],
            send_sem=send_sem.at[1 if down else 2], recv_sem=halo_recv.at[g, slot],
            device_id=(me, row_dev + 1 if down else row_dev - 1), device_id_type=MESH,
        )

    def each_group(d, use):
        for g in range(n):
            pl.when(groups[d] == g)(functools.partial(use, g))

    def forward(d, tile, part):
        first, count, slot = part

        def use(g):
            runs = runs_of(g * ep_local + first, count)

            @pl.when(has_below)
            def _():
                for run in runs:
                    halo_copy(True, run, tile, slot).start()

            @pl.when(has_above)
            def _():
                for run in runs:
                    halo_copy(False, run, tile, slot).start()

        each_group(d, use)

    def counting(rows, send, recv):
        return pltpu.make_async_remote_copy(
            src_ref=counted.at[pl.ds(0, rows)], dst_ref=counted.at[pl.ds(0, rows)],
            send_sem=send, recv_sem=recv, device_id=(groups[1], row_dev), device_id_type=MESH,
        )

    def wait_halo(g, part):
        first, count, slot = part
        rows = sum(2 * h * c for h, _, c in runs_of(g * ep_local + first, count))
        sem = halo_recv.at[g, slot]

        @pl.when(jnp.logical_and(has_above, has_below))
        def _():
            counting(2 * rows, send_sem.at[0], sem).wait_recv()

        @pl.when(has_above != has_below)
        def _():
            counting(rows, send_sem.at[0], sem).wait_recv()

    def clear_edges():
        for edge, refs in ((has_above, above), (has_below, below)):
            @pl.when(jnp.logical_not(edge))
            def _():
                for h, ref in refs.items():
                    for tile in range(tiles):
                        ref[tile] = jnp.zeros(ref.shape[1:], ref.dtype)

    first_row = jnp.where(has_above, -row_count, 0)
    end_row = jnp.where(has_below, 2 * row_count, row_count)

    def in_sky(row, size=BSUB):
        rows = lax.broadcasted_iota(jnp.int32, (size, LANES), 0) + row
        return jnp.logical_and(rows >= first_row, rows < end_row)

    def shift_of(level, index):
        number = shift_num[level, index]
        big = 2 * VMAX * 2**LEVELS
        whole = lax.div(number + DEN * big, DEN) - big
        left = number - whole * DEN
        fraction = left.astype(jnp.float32) / DEN
        return whole, whole + jnp.where(left > 0, 1, 0), fraction

    kinds = {}
    for blocks, _ in plans:
        for e, t, lane0, row0, size in blocks:
            key = (row0 - lane0, lane0 if lane0 else 0, bool(lane0))
            kinds.setdefault(key, len(kinds))

    def make_toeplitz():
        w = [psf_rows[b] for b in range(2 * reach + 1)]
        squares = [s * s for s in w]
        column = lax.broadcasted_iota(jnp.int32, (BSUB, LANES), 1)
        line = lax.broadcasted_iota(jnp.int32, (BSUB, LANES), 0)

        def body(b, carry):
            row = b * BSUB - row_count
            to = pl.multiple_of(b * BSUB, BSUB)
            keep = in_sky(row)
            for (offset, lane0, extra), at in kinds.items():
                tap = column - line - row + (offset + reach)
                ok = jnp.logical_and(keep, column >= lane0) if extra else keep
                tap = jnp.where(ok, tap, -1)
                for m, weights in enumerate((w, squares)):
                    value = jnp.zeros((BSUB, LANES), jnp.float32)
                    for a, weight in enumerate(weights):
                        value = jnp.where(tap == a, weight, value)
                    toeplitz[m, at, pl.ds(to, BSUB), :] = value
            return carry

        lax.fori_loop(0, 3 * row_count // BSUB, body, 0)

    def pad_of(g):
        return round_up(VMAX * g * ep_local, SUB)

    def mix(load, at, shift):
        near, far, fraction = shift
        return (1.0 - fraction) * load(at - near) + fraction * load(at - far)

    def make_matrix(g):
        base = g * ep_local
        blocks, used = plans[g]
        depth = len(used) * LANES

        def plane(ref, index):
            return lambda m: lambda at: ref[m, index, pl.ds(at, BSUB), :]

        state = []
        for e in range(ep_local):
            mine = {}
            for b, (epoch, t, lane0, row0, size) in enumerate(blocks):
                if epoch == e:
                    kind = kinds[(row0 - lane0, lane0, bool(lane0))]
                    mine[b] = (("toeplitz", kind), plane(toeplitz, kind))
            state.append(mine)
        planes = 0
        for level in range(local_levels - 1):
            half = 2**level
            made, following = [], [None] * ep_local
            for j in range(ep_local):
                if j & half:
                    continue
                for i in (j, j + half):
                    following[i] = dict(state[j])
                    for b, (_, source) in state[j + half].items():
                        made.append((planes, source, shift_of(level, base + i)))
                        following[i][b] = (("mid", planes), plane(mid, planes))
                        planes += 1
            pad = max(
                round_up(VMAX * (base + (j - j % (2 * half))), SUB) for j in range(ep_local)
            )

            def body(b, carry):
                row = b * BSUB - pad
                at = pl.multiple_of(row_count + row, SUB)
                keep = in_sky(row)
                for to, source, shift in made:
                    for m in range(2):
                        value = mix(source(m), at, shift)
                        mid[m, to, pl.ds(at, BSUB), :] = jnp.where(keep, value, 0.0)
                return carry

            lax.fori_loop(0, (row_count + 2 * pad) // BSUB, body, 0)
            state = following

        level = local_levels - 1
        half = 2**level
        pad = pad_of(g)
        size = row_count + 2 * pad
        entries = {}
        for j in range(half):
            for i in (j, j + half):
                for t in range(len(used)):
                    key = tuple(
                        (b, name, None) for b, (name, _) in state[j].items() if blocks[b][1] == t
                    ) + tuple(
                        (b, name, i) for b, (name, _) in state[j + half].items() if blocks[b][1] == t
                    )
                    entries.setdefault((t, key), []).append(i)
        sources = {name: source for mine in state for name, source in mine.values()}
        shifts = [shift_of(level, base + i) for i in range(ep_local)]
        ref = matrices[g]

        def body(b, carry):
            row = b * BSUB - pad
            at = pl.multiple_of(row_count + row, SUB)
            keep = in_sky(row)
            for (t, key), places in entries.items():
                for m in range(2):
                    value = None
                    for _, name, i in key:
                        load = sources[name](m)
                        part = load(at) if i is None else mix(load, at, shifts[i])
                        if i is not None:
                            part = jnp.where(keep, part, 0.0)
                        value = part if value is None else value + part
                    high = value.astype(jnp.bfloat16)
                    low = (value - high.astype(jnp.float32)).astype(jnp.bfloat16)
                    for i in places:
                        to = pl.multiple_of(i * size + b * BSUB, BSUB)
                        ref[m, pl.ds(to, BSUB), t * LANES:(t + 1) * LANES] = high
                        ref[m, pl.ds(to, BSUB), depth + t * LANES:depth + (t + 1) * LANES] = low
            return carry

        lax.fori_loop(0, size // BSUB, body, 0)

    def gather_rows(g, tile, m):
        blocks, used = plans[g]
        parts = []
        for t, filled in enumerate(used):
            for e, at, lane0, row0, size in sorted(blocks, key=lambda b: b[2]):
                if at != t:
                    continue
                epoch = g * ep_local + e
                h = halo_of(epoch)
                index = epoch - classes[h][0]
                row, end = row0, row0 + size
                if row < 0:
                    parts.append(above[h][tile, index, m, row + h:min(end, 0) + h, :])
                    row = min(end, 0)
                if row < min(end, row_count):
                    parts.append(pieces[g, tile, e, m, row:min(end, row_count), :])
                    row = min(end, row_count)
                if row < end:
                    parts.append(below[h][tile, index, m, row - row_count:end - row_count, :])
            if filled < LANES:
                parts.append(jnp.zeros((LANES - filled, LANES), jnp.bfloat16))
        return jnp.concatenate(parts, axis=0)

    def stack_group(g, tile):
        pad = pad_of(g)
        size = row_count + 2 * pad
        for m in range(2):
            x = gather_rows(g, tile, m)
            x = jnp.concatenate([x, x], axis=0)
            y = jnp.dot(matrices[g][m], x, preferred_element_type=jnp.float32)
            for i in range(ep_local):
                wide[0][g * ep_local + i, m, row_count - pad:row_count + row_count + pad, :] = (
                    y[i * size:(i + 1) * size]
                )

    def level_pass(level, src, dest, first):
        half = 2**level
        pad = round_up(VMAX * first, SUB)
        start, size = row_count - pad, row_count + 2 * pad
        if pad:
            lines = lax.broadcasted_iota(jnp.int32, (size, LANES), 0) - pad
            keep = jnp.logical_and(lines >= first_row, lines < end_row)
        for j in range(first, first + half):
            for i in (j, j + half):
                near, far, fraction = shift_of(level, i)
                for m in range(2):
                    x = src[j + half, m, pl.ds(start - near, size), :]
                    y = src[j + half, m, pl.ds(start - far, size), :]
                    value = src[j, m, start:start + size, :] + ((1.0 - fraction) * x + fraction * y)
                    dest[i, m, start:start + size, :] = jnp.where(keep, value, 0.0) if pad else value

    def finish(tile):
        for level in range(local_levels, LEVELS - 1):
            for first in range(0, epochs, 2 ** (level + 1)):
                level_pass(level, wide[level - local_levels], wide[level - local_levels + 1], first)
        final = wide[LEVELS - 1 - local_levels]
        half = epochs // 2
        shifts = [shift_of(LEVELS - 1, i) for i in range(epochs)]
        for row in range(0, row_count, FINAL):
            at = row_count + row
            likelihood = [None] * epochs
            for j in range(half):
                lower = [final[j, m, at:at + FINAL, :] for m in range(2)]
                for index in (j, j + half):
                    near, far, fraction = shifts[index]
                    maps = []
                    for m in range(2):
                        x = final[j + half, m, pl.ds(at - near, FINAL), :]
                        y = final[j + half, m, pl.ds(at - far, FINAL), :]
                        maps.append(lower[m] + ((1.0 - fraction) * x + fraction * y))
                    likelihood[index] = maps[0] * lax.rsqrt(maps[1])
            peak = functools.reduce(jnp.maximum, likelihood)
            total = functools.reduce(jnp.add, [jnp.exp(x - peak) for x in likelihood])
            out[row:row + FINAL, tile * LANES:(tile + 1) * LANES] = peak + jnp.log(total)

    loads[0].wait()
    make_bands()
    for load in loads[1:]:
        load.wait()
    order = send_order(n)
    first_core = lax.rem(row_dev, 2) == 0
    for tile in range(tiles):
        for d in order:
            filter_cols(groups[d], tile, outgoing.at[d - 1, tile] if d else pieces.at[me, tile])
            if tile == 0 and d == order[0]:
                near = jnp.where(has_above, 1, 0) + jnp.where(has_below, 1, 0)
                pl.semaphore_wait(barrier, n - 1 + near)
            if d:
                @pl.when(first_core)
                def _():
                    piece_copy(d, tile, parts_of(tile, tiles, ep_local)[0], me).start()

        parts = parts_of(tile, tiles, ep_local)

        @pl.when(first_core)
        def _():
            for part in parts[1:]:
                for d in order[:-1]:
                    piece_copy(d, tile, part, me).start()

        if tile >= HOLD or tile == tiles - 1:
            @pl.when(jnp.logical_not(first_core))
            def _():
                for now in range(tile + 1) if tile == min(HOLD, tiles - 1) else [tile]:
                    for part in parts_of(now, tiles, ep_local):
                        for d in order[:-1]:
                            piece_copy(d, now, part, me).start()

        for part in parts:
            forward(0, tile, part)

    clear_edges()
    make_toeplitz()
    for g in range(n):
        make_matrix(g)

    def stack_tile(g, tile):
        for part in parts_of(tile, tiles, ep_local):
            wait_halo(g, part)
        stack_group(g, tile)

    for tile in range(tiles):
        for part in parts_of(tile, tiles, ep_local):
            for d in order[:-1]:
                piece_copy(d, tile, part, groups[d]).wait_recv()
                forward(d, tile, part)
        if tile:
            for g in range(n):
                stack_tile(g, tile - 1)
            finish(tile - 1)
    for d in [0] + order[:-1]:
        each_group(d, functools.partial(stack_tile, tile=tiles - 1))
    finish(tiles - 1)

    pltpu.make_async_remote_copy(
        src_ref=outgoing, dst_ref=pieces.at[pl.ds(0, n - 1)], send_sem=send_sem.at[0],
        recv_sem=recv_sem.at[0, 0], device_id=(groups[1], row_dev), device_id_type=MESH,
    ).wait_send()
    for edge, sem in ((has_below, send_sem.at[1]), (has_above, send_sem.at[2])):
        @pl.when(edge)
        def _():
            counting(counted.shape[0], sem, recv_sem.at[0, 0]).wait_send()


def on_device(n, sky, image, inv_variance, psf_rows, psf_cols, shift_num):
    ep_local, row_count, cols = image.shape
    tiles = cols // n // LANES
    epochs = n * ep_local
    local_levels = ep_local.bit_length() - 1
    piece = (tiles, ep_local, 2, row_count, LANES)
    classes = classes_of(epochs)
    plans = [plan_of(g, ep_local, row_count) for g in range(n)]
    kinds = {(b[3] - b[2], b[2]) for blocks, _ in plans for b in blocks}
    halo_rows = sum(2 * tiles * halo_of(e) for e in range(epochs))
    halos = [
        pltpu.VMEM((tiles, count, 2, h, LANES), jnp.bfloat16) for h, (_, count) in classes.items()
    ]
    matrices = []
    for g in range(n):
        size = row_count + 2 * round_up(VMAX * g * ep_local, SUB)
        depth = 2 * LANES * len(plans[g][1])
        matrices.append(pltpu.VMEM((2, ep_local * size, depth), jnp.bfloat16))
    most = max(len(blocks) for blocks, _ in plans)

    any_space = pl.BlockSpec(memory_space=pl.ANY)
    vmem = pl.BlockSpec(memory_space=pltpu.VMEM)
    return pl.pallas_call(
        functools.partial(kernel, n, sky),
        out_shape=pltpu.VMEM((row_count, cols // n), jnp.float32),
        in_specs=[any_space] * 5,
        out_specs=vmem,
        scratch_shapes=[
            pltpu.VMEM(image.shape, jnp.bfloat16),
            pltpu.VMEM(image.shape, jnp.bfloat16),
            pltpu.SMEM(psf_rows.shape, jnp.float32),
            pltpu.SMEM(psf_cols.shape, jnp.float32),
            pltpu.SMEM(shift_num.shape, jnp.int32),
            pltpu.VMEM((n - 1,) + piece, jnp.bfloat16),
            pltpu.VMEM((n,) + piece, jnp.bfloat16),
            pltpu.VMEM((2, 2 * LANES, 2 * LANES), jnp.bfloat16),
            pltpu.VMEM((2, len(kinds), 3 * row_count, LANES), jnp.float32),
            pltpu.VMEM((2, max(1, local_levels * most), 3 * row_count, LANES), jnp.float32),
            pltpu.VMEM((halo_rows, LANES), jnp.bfloat16),
        ]
        + halos + halos + matrices
        + [
            pltpu.VMEM((epochs, 2, 3 * row_count, LANES), jnp.float32)
            for _ in range(LEVELS - local_levels)
        ]
        + [
            pltpu.SemaphoreType.DMA((5,)),
            pltpu.SemaphoreType.DMA((3,)),
            pltpu.SemaphoreType.DMA((n - 1, tiles + 1)),
            pltpu.SemaphoreType.DMA((n, tiles + 1)),
        ],
        compiler_params=pltpu.CompilerParams(
            collective_id=0, has_side_effects=True, vmem_limit_bytes=60 * 1024 * 1024
        ),
    )(image, inv_variance, psf_rows, psf_cols, shift_num)


def solution(mesh):
    body = functools.partial(on_device, mesh.shape["epoch"], mesh.shape["sky"])
    return jax.shard_map(
        body,
        mesh=mesh,
        in_specs=(P("epoch", "sky", None), P("epoch", "sky", None), P(), P(), P()),
        out_specs=P("sky", "epoch"),
        check_vma=False,
    )
```

```python
import functools

import jax
import jax.numpy as jnp
from jax import lax
from jax.experimental import pallas as pl
from jax.experimental.pallas import tpu as pltpu
from jax.sharding import PartitionSpec as P

LEVELS = 4
PSF_HALF = 4
DEN = 4
VMAX = 2
LANES = 128
SUB = 8
BSUB = 16
FINAL = 16
HOLD = 1
MESH = pl.DeviceIdType.MESH


def flip(index, mask, size):
    result, bit = 0, 1
    while bit < size:
        digit = lax.rem(lax.div(index, bit), 2)
        result = result + bit * ((1 - digit) if mask & bit else digit)
        bit *= 2
    return result


def round_up(value, step):
    return (value + step - 1) // step * step


def halo_of(epoch):
    return round_up(VMAX * epoch + PSF_HALF, BSUB)


def classes_of(epochs):
    found = {}
    for e in range(epochs):
        first, count = found.get(halo_of(e), (e, 0))
        found[halo_of(e)] = (first, count + 1)
    return found


def runs_of(start, count):
    runs = []
    for e in range(start, start + count):
        if runs and runs[-1][0] == halo_of(e):
            runs[-1] = (runs[-1][0], runs[-1][1], runs[-1][2] + 1)
        else:
            runs.append((halo_of(e), e, 1))
    return runs


def plan_of(g, ep_local, row_count):
    blocks, used, left = [], [], []
    for e in range(ep_local):
        h = halo_of(g * ep_local + e)
        size = row_count + 2 * h
        first = min(size, LANES)
        blocks.append((e, len(used), 0, -h, first))
        used.append(first)
        if size > first:
            left.append((e, first - h, size - first))
    for e, row, size in left:
        at = next((t for t, u in enumerate(used) if u + size <= LANES), None)
        if at is None:
            at = len(used)
            used.append(0)
        blocks.append((e, at, used[at], row, size))
        used[at] += size
    return blocks, used


def send_order(n):
    return sorted(range(1, n), key=lambda d: (-bin(d).count("1"), d)) + [0]


def parts_of(tile, tiles, ep_local):
    if tile < tiles - 1 or ep_local == 1:
        return [(0, ep_local, tile)]
    half = ep_local // 2
    return [(half, ep_local - half, tile), (0, half, tiles)]


def kernel(
    n, sky, image_hbm, variance_hbm, psf_rows_hbm, psf_cols_hbm, shift_hbm, out,
    image, variance, psf_rows, psf_cols, shift_num,
    outgoing, pieces, bands, toeplitz, mid, counted, *rest,
):
    ep_local, row_count = image.shape[0], image.shape[1]
    epochs = n * ep_local
    tiles = image.shape[2] // n // LANES
    reach = PSF_HALF
    local_levels = ep_local.bit_length() - 1
    classes = classes_of(epochs)
    plans = [plan_of(g, ep_local, row_count) for g in range(n)]
    rest = list(rest)
    above = {h: rest.pop(0) for h in classes}
    below = {h: rest.pop(0) for h in classes}
    matrices = [rest.pop(0) for _ in range(n)]
    wide = [rest.pop(0) for _ in range(LEVELS - local_levels)]
    in_sem, send_sem, recv_sem, halo_recv = rest

    me = lax.axis_index("epoch")
    row_dev = lax.axis_index("sky")
    has_above = row_dev > 0
    has_below = row_dev < sky - 1
    groups = [flip(me, d, n) for d in range(n)]

    barrier = pltpu.get_barrier_semaphore()
    for d in range(1, n):
        pl.semaphore_signal(barrier, inc=1, device_id=(groups[d], row_dev), device_id_type=MESH)

    @pl.when(has_above)
    def _():
        pl.semaphore_signal(barrier, inc=1, device_id=(me, row_dev - 1), device_id_type=MESH)

    @pl.when(has_below)
    def _():
        pl.semaphore_signal(barrier, inc=1, device_id=(me, row_dev + 1), device_id_type=MESH)

    whole = (
        (psf_cols_hbm, psf_cols), (image_hbm, image), (variance_hbm, variance),
        (psf_rows_hbm, psf_rows), (shift_hbm, shift_num),
    )
    loads = [pltpu.make_async_copy(a, b, in_sem.at[i]) for i, (a, b) in enumerate(whole)]
    for load in loads:
        load.start()

    def make_bands():
        source = lax.broadcasted_iota(jnp.int32, (2 * LANES, LANES), 0)
        column = lax.broadcasted_iota(jnp.int32, (2 * LANES, LANES), 1)
        at = jnp.where(source < LANES + LANES // 2, source, source - 2 * LANES)
        tap = at - column + reach
        for m in range(2):
            band = jnp.zeros((2 * LANES, LANES), jnp.float32)
            for b in range(2 * reach + 1):
                weight = psf_cols[b] if m == 0 else psf_cols[b] * psf_cols[b]
                band = jnp.where(tap == b, weight, band)
            high = band.astype(jnp.bfloat16)
            bands[m, :, :LANES] = high
            bands[m, :, LANES:] = (band - high.astype(jnp.float32)).astype(jnp.bfloat16)

    lane = lax.broadcasted_iota(jnp.int32, (ep_local * row_count, LANES), 1)

    def filter_cols(p, tile, dest):
        here = p * tiles + tile
        flat = (ep_local * row_count, LANES)

        def take(ref, t):
            at = pl.multiple_of(t * LANES, LANES)
            return ref[:, :, pl.ds(at, LANES)].astype(jnp.float32).reshape(flat)

        def both(t, keep):
            v = take(variance, t)
            if keep is not None:
                v = v * keep
            return take(image, t) * v, v

        total = n * tiles
        left_on = jnp.where(here > 0, 1.0, 0.0).astype(jnp.float32)
        right_on = jnp.where(here < total - 1, 1.0, 0.0).astype(jnp.float32)
        left = both(jnp.maximum(here - 1, 0), left_on)
        centre = both(here, None)
        right = both(jnp.minimum(here + 1, total - 1), right_on)
        for m in range(2):
            edge = jnp.where(lane < LANES // 2, right[m], left[m])
            x = jnp.concatenate([centre[m], edge], axis=1)
            high = x.astype(jnp.bfloat16)
            y = jnp.dot(high, bands[m], preferred_element_type=jnp.float32)
            y = y[:, :LANES] + y[:, LANES:]
            if m == 0:
                low = (x - high.astype(jnp.float32)).astype(jnp.bfloat16)
                y = y + jnp.dot(low, bands[m, :, :LANES], preferred_element_type=jnp.float32)
            dest[:, m] = y.reshape(ep_local, row_count, LANES).astype(jnp.bfloat16)

    def piece_copy(d, tile, part, group):
        first, count, slot = part
        epochs_of = pl.ds(first, count)
        return pltpu.make_async_remote_copy(
            src_ref=outgoing.at[d - 1, tile, epochs_of], dst_ref=pieces.at[group, tile, epochs_of],
            send_sem=send_sem.at[0], recv_sem=recv_sem.at[d - 1, slot],
            device_id=(groups[d], row_dev), device_id_type=MESH,
        )

    def halo_sem(g, slot):
        last = tiles - 1
        return halo_recv.at[slot if slot < last else last + 2 * g + slot - last]

    def halo_copy(down, run, tile, slot):
        h, start, count = run
        g = start // ep_local
        at = start - classes[h][0]
        rows = pl.ds(row_count - h, h) if down else pl.ds(0, h)
        return pltpu.make_async_remote_copy(
            src_ref=pieces.at[g, tile, pl.ds(start - g * ep_local, count), :, rows, :],
            dst_ref=(above if down else below)[h].at[tile, pl.ds(at, count)],
            send_sem=send_sem.at[1 if down else 2], recv_sem=halo_sem(g, slot),
            device_id=(me, row_dev + 1 if down else row_dev - 1), device_id_type=MESH,
        )

    def each_group(d, use):
        for g in range(n):
            pl.when(groups[d] == g)(functools.partial(use, g))

    def forward(d, tile, part):
        first, count, slot = part

        def use(g):
            runs = runs_of(g * ep_local + first, count)

            @pl.when(has_below)
            def _():
                for run in runs:
                    halo_copy(True, run, tile, slot).start()

            @pl.when(has_above)
            def _():
                for run in runs:
                    halo_copy(False, run, tile, slot).start()

        each_group(d, use)

    def counting(rows, send, recv):
        return pltpu.make_async_remote_copy(
            src_ref=counted.at[pl.ds(0, rows)], dst_ref=counted.at[pl.ds(0, rows)],
            send_sem=send, recv_sem=recv, device_id=(groups[1], row_dev), device_id_type=MESH,
        )

    def wait_halo(which, part):
        first, count, slot = part
        rows = sum(2 * h * c for g in which for h, _, c in runs_of(g * ep_local + first, count))
        sem = halo_sem(which[0], slot)

        @pl.when(jnp.logical_and(has_above, has_below))
        def _():
            counting(2 * rows, send_sem.at[0], sem).wait_recv()

        @pl.when(has_above != has_below)
        def _():
            counting(rows, send_sem.at[0], sem).wait_recv()

    def clear_edges():
        for edge, refs in ((has_above, above), (has_below, below)):
            @pl.when(jnp.logical_not(edge))
            def _():
                for h, ref in refs.items():
                    for tile in range(tiles):
                        ref[tile] = jnp.zeros(ref.shape[1:], ref.dtype)

    first_row = jnp.where(has_above, -row_count, 0)
    end_row = jnp.where(has_below, 2 * row_count, row_count)

    def in_sky(row, size=BSUB):
        rows = lax.broadcasted_iota(jnp.int32, (size, LANES), 0) + row
        return jnp.logical_and(rows >= first_row, rows < end_row)

    def shift_of(level, index):
        number = shift_num[level, index]
        big = 2 * VMAX * 2**LEVELS
        whole = lax.div(number + DEN * big, DEN) - big
        left = number - whole * DEN
        fraction = left.astype(jnp.float32) / DEN
        return whole, whole + jnp.where(left > 0, 1, 0), fraction

    kinds = {}
    for blocks, _ in plans:
        for e, t, lane0, row0, size in blocks:
            key = (row0 - lane0, lane0 if lane0 else 0, bool(lane0))
            kinds.setdefault(key, len(kinds))

    def make_toeplitz():
        w = [psf_rows[b] for b in range(2 * reach + 1)]
        squares = [s * s for s in w]
        column = lax.broadcasted_iota(jnp.int32, (BSUB, LANES), 1)
        line = lax.broadcasted_iota(jnp.int32, (BSUB, LANES), 0)

        def body(b, carry):
            row = b * BSUB - row_count
            to = pl.multiple_of(b * BSUB, BSUB)
            keep = in_sky(row)
            for (offset, lane0, extra), at in kinds.items():
                tap = column - line - row + (offset + reach)
                ok = jnp.logical_and(keep, column >= lane0) if extra else keep
                tap = jnp.where(ok, tap, -1)
                for m, weights in enumerate((w, squares)):
                    value = jnp.zeros((BSUB, LANES), jnp.float32)
                    for a, weight in enumerate(weights):
                        value = jnp.where(tap == a, weight, value)
                    toeplitz[m, at, pl.ds(to, BSUB), :] = value
            return carry

        lax.fori_loop(0, 3 * row_count // BSUB, body, 0)

    def pad_of(g):
        return round_up(VMAX * g * ep_local, SUB)

    def mix(load, at, shift):
        near, far, fraction = shift
        return (1.0 - fraction) * load(at - near) + fraction * load(at - far)

    def make_matrix(g):
        base = g * ep_local
        blocks, used = plans[g]
        depth = len(used) * LANES

        def plane(ref, index):
            return lambda m: lambda at: ref[m, index, pl.ds(at, BSUB), :]

        state = []
        for e in range(ep_local):
            mine = {}
            for b, (epoch, t, lane0, row0, size) in enumerate(blocks):
                if epoch == e:
                    kind = kinds[(row0 - lane0, lane0, bool(lane0))]
                    mine[b] = (("toeplitz", kind), plane(toeplitz, kind))
            state.append(mine)
        planes = 0
        for level in range(local_levels - 1):
            half = 2**level
            made, following = [], [None] * ep_local
            for j in range(ep_local):
                if j & half:
                    continue
                for i in (j, j + half):
                    following[i] = dict(state[j])
                    for b, (_, source) in state[j + half].items():
                        made.append((planes, source, shift_of(level, base + i)))
                        following[i][b] = (("mid", planes), plane(mid, planes))
                        planes += 1
            pad = max(
                round_up(VMAX * (base + (j - j % (2 * half))), SUB) for j in range(ep_local)
            )

            def body(b, carry):
                row = b * BSUB - pad
                at = pl.multiple_of(row_count + row, SUB)
                keep = in_sky(row)
                for to, source, shift in made:
                    for m in range(2):
                        value = mix(source(m), at, shift)
                        mid[m, to, pl.ds(at, BSUB), :] = jnp.where(keep, value, 0.0)
                return carry

            lax.fori_loop(0, (row_count + 2 * pad) // BSUB, body, 0)
            state = following

        level = local_levels - 1
        half = 2**level
        pad = pad_of(g)
        size = row_count + 2 * pad
        entries = {}
        for j in range(half):
            for i in (j, j + half):
                for t in range(len(used)):
                    key = tuple(
                        (b, name, None) for b, (name, _) in state[j].items() if blocks[b][1] == t
                    ) + tuple(
                        (b, name, i) for b, (name, _) in state[j + half].items() if blocks[b][1] == t
                    )
                    entries.setdefault((t, key), []).append(i)
        sources = {name: source for mine in state for name, source in mine.values()}
        shifts = [shift_of(level, base + i) for i in range(ep_local)]
        ref = matrices[g]

        def body(b, carry):
            row = b * BSUB - pad
            at = pl.multiple_of(row_count + row, SUB)
            keep = in_sky(row)
            for (t, key), places in entries.items():
                for m in range(2):
                    value = None
                    for _, name, i in key:
                        load = sources[name](m)
                        part = load(at) if i is None else mix(load, at, shifts[i])
                        if i is not None:
                            part = jnp.where(keep, part, 0.0)
                        value = part if value is None else value + part
                    high = value.astype(jnp.bfloat16)
                    low = (value - high.astype(jnp.float32)).astype(jnp.bfloat16)
                    for i in places:
                        to = pl.multiple_of(i * size + b * BSUB, BSUB)
                        ref[m, pl.ds(to, BSUB), t * LANES:(t + 1) * LANES] = high
                        ref[m, pl.ds(to, BSUB), depth + t * LANES:depth + (t + 1) * LANES] = low
            return carry

        lax.fori_loop(0, size // BSUB, body, 0)

    def gather_rows(g, tile, m):
        blocks, used = plans[g]
        parts = []
        for t, filled in enumerate(used):
            for e, at, lane0, row0, size in sorted(blocks, key=lambda b: b[2]):
                if at != t:
                    continue
                epoch = g * ep_local + e
                h = halo_of(epoch)
                index = epoch - classes[h][0]
                row, end = row0, row0 + size
                if row < 0:
                    parts.append(above[h][tile, index, m, row + h:min(end, 0) + h, :])
                    row = min(end, 0)
                if row < min(end, row_count):
                    parts.append(pieces[g, tile, e, m, row:min(end, row_count), :])
                    row = min(end, row_count)
                if row < end:
                    parts.append(below[h][tile, index, m, row - row_count:end - row_count, :])
            if filled < LANES:
                parts.append(jnp.zeros((LANES - filled, LANES), jnp.bfloat16))
        return jnp.concatenate(parts, axis=0)

    def stack_group(g, tile):
        pad = pad_of(g)
        size = row_count + 2 * pad
        for m in range(2):
            x = gather_rows(g, tile, m)
            x = jnp.concatenate([x, x], axis=0)
            y = jnp.dot(matrices[g][m], x, preferred_element_type=jnp.float32)
            for i in range(ep_local):
                wide[0][g * ep_local + i, m, row_count - pad:row_count + row_count + pad, :] = (
                    y[i * size:(i + 1) * size]
                )

    def level_pass(level, src, dest, first):
        half = 2**level
        pad = round_up(VMAX * first, SUB)
        start, size = row_count - pad, row_count + 2 * pad
        if pad:
            lines = lax.broadcasted_iota(jnp.int32, (size, LANES), 0) - pad
            keep = jnp.logical_and(lines >= first_row, lines < end_row)
        for j in range(first, first + half):
            for i in (j, j + half):
                near, far, fraction = shift_of(level, i)
                for m in range(2):
                    x = src[j + half, m, pl.ds(start - near, size), :]
                    y = src[j + half, m, pl.ds(start - far, size), :]
                    value = src[j, m, start:start + size, :] + ((1.0 - fraction) * x + fraction * y)
                    dest[i, m, start:start + size, :] = jnp.where(keep, value, 0.0) if pad else value

    def finish(tile):
        for level in range(local_levels, LEVELS - 1):
            for first in range(0, epochs, 2 ** (level + 1)):
                level_pass(level, wide[level - local_levels], wide[level - local_levels + 1], first)
        final = wide[LEVELS - 1 - local_levels]
        half = epochs // 2
        shifts = [shift_of(LEVELS - 1, i) for i in range(epochs)]
        for row in range(0, row_count, FINAL):
            at = row_count + row
            likelihood = [None] * epochs
            for j in range(half):
                lower = [final[j, m, at:at + FINAL, :] for m in range(2)]
                for index in (j, j + half):
                    near, far, fraction = shifts[index]
                    maps = []
                    for m in range(2):
                        x = final[j + half, m, pl.ds(at - near, FINAL), :]
                        y = final[j + half, m, pl.ds(at - far, FINAL), :]
                        maps.append(lower[m] + ((1.0 - fraction) * x + fraction * y))
                    likelihood[index] = maps[0] * lax.rsqrt(maps[1])
            peak = functools.reduce(jnp.maximum, likelihood)
            total = functools.reduce(jnp.add, [jnp.exp(x - peak) for x in likelihood])
            out[row:row + FINAL, tile * LANES:(tile + 1) * LANES] = peak + jnp.log(total)

    loads[0].wait()
    make_bands()
    for load in loads[1:]:
        load.wait()
    order = send_order(n)
    first_core = lax.rem(row_dev, 2) == 0
    for tile in range(tiles):
        for d in order:
            filter_cols(groups[d], tile, outgoing.at[d - 1, tile] if d else pieces.at[me, tile])
            if tile == 0 and d == order[0]:
                near = jnp.where(has_above, 1, 0) + jnp.where(has_below, 1, 0)
                pl.semaphore_wait(barrier, n - 1 + near)
            if d:
                @pl.when(first_core)
                def _():
                    piece_copy(d, tile, parts_of(tile, tiles, ep_local)[0], me).start()

        parts = parts_of(tile, tiles, ep_local)

        @pl.when(first_core)
        def _():
            for part in parts[1:]:
                for d in order[:-1]:
                    piece_copy(d, tile, part, me).start()

        if tile >= HOLD or tile == tiles - 1:
            @pl.when(jnp.logical_not(first_core))
            def _():
                for now in range(tile + 1) if tile == min(HOLD, tiles - 1) else [tile]:
                    for part in parts_of(now, tiles, ep_local):
                        for d in order[:-1]:
                            piece_copy(d, now, part, me).start()

        for part in parts:
            forward(0, tile, part)

    clear_edges()
    make_toeplitz()
    for g in range(n):
        make_matrix(g)

    def stack_last(g):
        for part in parts_of(tiles - 1, tiles, ep_local):
            wait_halo([g], part)
        stack_group(g, tiles - 1)

    for tile in range(tiles):
        for part in parts_of(tile, tiles, ep_local):
            for d in order[:-1]:
                piece_copy(d, tile, part, groups[d]).wait_recv()
                forward(d, tile, part)
        if tile:
            for part in parts_of(tile - 1, tiles, ep_local):
                wait_halo(range(n), part)
            for g in range(n):
                stack_group(g, tile - 1)
            finish(tile - 1)
    for d in [0] + order[:-1]:
        each_group(d, stack_last)
    finish(tiles - 1)

    pltpu.make_async_remote_copy(
        src_ref=outgoing, dst_ref=pieces.at[pl.ds(0, n - 1)], send_sem=send_sem.at[0],
        recv_sem=recv_sem.at[0, 0], device_id=(groups[1], row_dev), device_id_type=MESH,
    ).wait_send()
    for edge, sem in ((has_below, send_sem.at[1]), (has_above, send_sem.at[2])):
        @pl.when(edge)
        def _():
            counting(counted.shape[0], sem, recv_sem.at[0, 0]).wait_send()


def on_device(n, sky, image, inv_variance, psf_rows, psf_cols, shift_num):
    ep_local, row_count, cols = image.shape
    tiles = cols // n // LANES
    epochs = n * ep_local
    local_levels = ep_local.bit_length() - 1
    piece = (tiles, ep_local, 2, row_count, LANES)
    classes = classes_of(epochs)
    plans = [plan_of(g, ep_local, row_count) for g in range(n)]
    kinds = {(b[3] - b[2], b[2]) for blocks, _ in plans for b in blocks}
    halo_rows = sum(2 * tiles * halo_of(e) for e in range(epochs))
    halos = [
        pltpu.VMEM((tiles, count, 2, h, LANES), jnp.bfloat16) for h, (_, count) in classes.items()
    ]
    matrices = []
    for g in range(n):
        size = row_count + 2 * round_up(VMAX * g * ep_local, SUB)
        depth = 2 * LANES * len(plans[g][1])
        matrices.append(pltpu.VMEM((2, ep_local * size, depth), jnp.bfloat16))
    most = max(len(blocks) for blocks, _ in plans)

    any_space = pl.BlockSpec(memory_space=pl.ANY)
    vmem = pl.BlockSpec(memory_space=pltpu.VMEM)
    return pl.pallas_call(
        functools.partial(kernel, n, sky),
        out_shape=pltpu.VMEM((row_count, cols // n), jnp.float32),
        in_specs=[any_space] * 5,
        out_specs=vmem,
        scratch_shapes=[
            pltpu.VMEM(image.shape, jnp.bfloat16),
            pltpu.VMEM(image.shape, jnp.bfloat16),
            pltpu.SMEM(psf_rows.shape, jnp.float32),
            pltpu.SMEM(psf_cols.shape, jnp.float32),
            pltpu.SMEM(shift_num.shape, jnp.int32),
            pltpu.VMEM((n - 1,) + piece, jnp.bfloat16),
            pltpu.VMEM((n,) + piece, jnp.bfloat16),
            pltpu.VMEM((2, 2 * LANES, 2 * LANES), jnp.bfloat16),
            pltpu.VMEM((2, len(kinds), 3 * row_count, LANES), jnp.float32),
            pltpu.VMEM((2, max(1, local_levels * most), 3 * row_count, LANES), jnp.float32),
            pltpu.VMEM((halo_rows, LANES), jnp.bfloat16),
        ]
        + halos + halos + matrices
        + [
            pltpu.VMEM((epochs, 2, 3 * row_count, LANES), jnp.float32)
            for _ in range(LEVELS - local_levels)
        ]
        + [
            pltpu.SemaphoreType.DMA((5,)),
            pltpu.SemaphoreType.DMA((3,)),
            pltpu.SemaphoreType.DMA((n - 1, tiles + 1)),
            pltpu.SemaphoreType.DMA((tiles - 1 + 2 * n,)),
        ],
        compiler_params=pltpu.CompilerParams(
            collective_id=0, has_side_effects=True, vmem_limit_bytes=60 * 1024 * 1024
        ),
    )(image, inv_variance, psf_rows, psf_cols, shift_num)


def solution(mesh):
    body = functools.partial(on_device, mesh.shape["epoch"], mesh.shape["sky"])
    return jax.shard_map(
        body,
        mesh=mesh,
        in_specs=(P("epoch", "sky", None), P("epoch", "sky", None), P(), P(), P()),
        out_specs=P("sky", "epoch"),
        check_vma=False,
    )
```
